32 devices in a mesh: sub: 8 (over y, x, core), row: 4 (over z).
Axes of the slice: x: 2, y: 2, z: 4, core: 2. Of those that a mesh axis runs over, the one named last changes fastest.
Arguments:
- band: float32 [16384, 1024], P(('sub', 'row')), parts along dimension 0, as said below
- precond: float32 [16384, 128], P(('sub', 'row')), parts along dimension 0, as said below
- half_band: int32 [8], P('sub'), parts along dimension 0, may hold values from 64 to 256
- interface: float32 [16384, 512], P(('sub', 'row')), parts along dimension 0, may hold values from -6 to 6
Outputs:
- modes: float32 [16384, 512], P(('sub', 'row')), parts along dimension 0
The draws below stay inside these ranges and needn't reach their ends.
There are 8 independent parts, one for each index of `sub`. The reference program is written for one: setup_inputs(seed, part) draws one part's arguments, and reference() takes and returns one part's arrays. A program takes and returns all parts, laid end to end along the dimension named above; each array names one. Nothing has to cross between parts.
Inputs may be any that keep to these rules, and one draw needn't show every extreme that they name: band is symmetric as a stiffness: the entry coupling rows r and s equals that coupling s and r; entries at offset 0 lie in 0.05 to 0.5; entries beyond offset 256 or outside the matrix are 0; all entries are nonnegative. `precond`: every block is a symmetric positive definite 128 x 128 matrix.
All inputs are finite; a program needn't handle non-finite values.
Results may differ from the reference program's by a relative error of at most 0.0001.
Values sent between devices are 32-bit elements; how exact they have to be, the bound alone decides.
A program may use at most 64 MiB of HBM per device.

```python
import math
import jax
import jax.numpy as jnp
from jax import lax

ROWS_DEV = 512
COLS = 512
BAND = 256
BLOCK = 128
ITERS = 3
INTERIOR = 2048
N_ROW = 4


def draw_band(key, part):
    first_key = jax.random.fold_in(key, 11)
    second_key = jax.random.fold_in(key, 12)
    weights = jax.random.uniform(first_key, (INTERIOR, BAND), jnp.float32, 0.5, 1.5) / BAND
    diag_shift = jnp.exp(jax.random.uniform(second_key, (INTERIOR,), jnp.float32, math.log(0.05), math.log(0.5)))
    width = ROWS_DEV + 2 * BAND
    row_ids = jnp.arange(INTERIOR, dtype=jnp.int32)[:, None]
    col_ids = jnp.arange(width, dtype=jnp.int32)[None, :]
    offsets = col_ids - BAND - row_ids % ROWS_DEV
    global_col = row_ids + offsets
    usable = (global_col >= 0) & (global_col < INTERIOR) & (jnp.abs(offsets) <= BAND) & (offsets != 0)
    lower_row = jnp.clip(jnp.minimum(row_ids, global_col), 0, INTERIOR - 1)
    lag_index = jnp.clip(jnp.abs(offsets) - 1, 0, BAND - 1)
    values = weights[lower_row, lag_index]
    values = jnp.where(usable, values, jnp.zeros_like(values))
    diag_full = jnp.broadcast_to(diag_shift[:, None], values.shape)
    return jnp.where(offsets == 0, diag_full, values).astype(jnp.float32)


def draw_precond(key, part):
    blocks = INTERIOR // BLOCK
    factors = jax.random.normal(jax.random.fold_in(key, 21), (blocks, BLOCK, BLOCK), jnp.float32)
    gram = jnp.einsum('bij,bkj->bik', factors, factors) * (0.15 / BLOCK)
    matrices = gram + 0.1 * jnp.eye(BLOCK, dtype=jnp.float32)[None, :, :]
    return matrices.reshape(INTERIOR, BLOCK).astype(jnp.float32)


def steps_of(stream_key, shape, split, smallest, high):
    level, own = 1.0, jax.random.fold_in(stream_key, 6)
    for position, shards_of in split:
        draws = jnp.exp(jax.random.uniform(jax.random.fold_in(own, position), (shards_of,), jnp.float32, smallest / len(split), high / len(split)))
        level = level * jnp.repeat(draws, shape[position] // shards_of).reshape([-1 if axis == position else 1 for axis in range(len(shape))])
    return level


def centred(rng, dims, deviation, bound, cuts=(), held_as=jnp.bfloat16):
    drawn = deviation * jax.random.normal(rng, dims, jnp.float32)
    if cuts:
        drawn = drawn * steps_of(rng, dims, cuts, -0.22, 0.18)
    return jnp.clip(drawn, -bound, bound).astype(held_as)


def setup_inputs(seed: int = 0, part: int = 0) -> dict:
    keys = jax.random.split(jax.random.key(seed), 5)
    part_keys = jax.random.split(jax.random.fold_in(keys[4], part), 5)
    band = draw_band(jax.random.fold_in(jax.random.fold_in(keys[4], part), 71), part)
    precond = draw_precond(jax.random.fold_in(jax.random.fold_in(keys[4], part), 71), part)
    half_band = jax.random.randint(part_keys[2], (1,), BAND // 4, BAND + 1).astype(jnp.int32)
    interface = centred(part_keys[3], (INTERIOR, COLS), 1.0, 6.0, ((0, 4),), jnp.float32)
    return dict(band=band, precond=precond, half_band=half_band, interface=interface)


def couplings(band, half_band):
    width = band.shape[1]
    local_rows = jnp.arange(band.shape[0], dtype=jnp.int32) % ROWS_DEV
    offsets = jnp.arange(width, dtype=jnp.int32)[None, :] - BAND - local_rows[:, None]
    reach = jnp.abs(offsets)
    inside = (reach >= 1) & (reach <= half_band[0])
    coupling = jnp.where(inside, band, jnp.zeros_like(band))
    diagonal = jnp.sum(coupling, axis=1) + jnp.sum(jnp.where(offsets == 0, band, jnp.zeros_like(band)), axis=1)
    return coupling, diagonal


def stiffness(vector, coupling, diagonal):
    width = ROWS_DEV + 2 * BAND
    padded = jnp.pad(vector, ((BAND, BAND), (0, 0)))
    stacked = coupling.reshape(N_ROW, ROWS_DEV, width)

    def one_block(index):
        window = lax.dynamic_slice_in_dim(padded, index * ROWS_DEV, width, 0)
        return jnp.dot(stacked[index], window, precision=lax.Precision.HIGHEST, preferred_element_type=jnp.float32)

    products = lax.map(one_block, jnp.arange(N_ROW, dtype=jnp.int32))
    return diagonal[:, None] * vector - products.reshape(vector.shape)


def precondition(vector, precond):
    blocks = vector.shape[0] // BLOCK
    matrices = precond.reshape(blocks, BLOCK, BLOCK)
    pieces = vector.reshape(blocks, BLOCK, vector.shape[1])
    return jnp.einsum("bij,bjm->bim", matrices, pieces, precision=lax.Precision.HIGHEST).reshape(vector.shape)


def reference(band, precond, half_band, interface):
    coupling, diagonal = couplings(band, half_band)
    residual = -interface
    modes = jnp.zeros_like(interface)
    precond_res = precondition(residual, precond)
    energy = jnp.sum(residual * precond_res, axis=0)
    direction = precond_res
    for iteration in range(ITERS):
        image = stiffness(direction, coupling, diagonal)
        step_len = energy / jnp.sum(direction * image, axis=0)
        modes = modes + step_len[None, :] * direction
        residual = residual - step_len[None, :] * image
        if iteration + 1 < ITERS:
            precond_res = precondition(residual, precond)
            energy_next = jnp.sum(residual * precond_res, axis=0)
            direction = precond_res + (energy_next / energy)[None, :] * direction
            energy = energy_next
    return modes
```

```python
import functools

import jax
import jax.numpy as jnp
from jax import lax
from jax.experimental import pallas as pl
from jax.experimental.pallas import tpu as pltpu
from jax.sharding import PartitionSpec as P

MESH = pl.DeviceIdType.MESH
CHUNK = 256
F32 = jnp.float32
BF16 = jnp.bfloat16


def split(value):
    high = value.astype(BF16)
    return high, (value - high.astype(F32)).astype(BF16)


def dot(left, right):
    return jnp.dot(left, right, preferred_element_type=F32)


def dot3(left_hi, left_lo, right_hi, right_lo):
    return dot(left_hi, right_hi) + dot(left_lo, right_hi) + dot(left_hi, right_lo)


def kernel(
    n,
    band_hbm,
    precond_hbm,
    half_ref,
    rhs_hbm,
    out_hbm,
    band,
    precond,
    rhs,
    out,
    chi,
    clo,
    pcat,
    diag,
    z0,
    w0,
    z1,
    w1,
    u,
    vhi,
    vlo,
    halo0,
    halo1,
    halo2,
    red0,
    red1,
    in_sem,
    out_sem,
    send_sem,
    recv_sem,
    rsend_sem,
    rrecv_sem,
):
    me = lax.axis_index("row")
    rows, width = band.shape
    edge = (width - rows) // 2
    block = precond.shape[1]
    chunks = rhs.shape[0]
    half = CHUNK // 2
    low_rows, high_rows = slice(0, edge), slice(rows - edge, rows)
    low_cols, mid_cols, high_cols = slice(0, edge), slice(edge, edge + rows), slice(edge + rows, width)

    loads = [pltpu.make_async_copy(precond_hbm, precond, in_sem.at[0])]
    for c in range(chunks):
        loads.append(
            pltpu.make_async_copy(
                rhs_hbm.at[:, pl.ds(c * CHUNK, CHUNK)], rhs.at[c], in_sem.at[2 + c]
            )
        )
    loads.append(pltpu.make_async_copy(band_hbm, band, in_sem.at[1]))
    for load in loads:
        load.start()

    barrier = pltpu.get_barrier_semaphore()
    for k in range(1, n):
        pl.semaphore_signal(
            barrier, inc=1, device_id={"row": lax.rem(me + k, n)}, device_id_type=MESH
        )

    def exchange(stage, c):
        if stage < 2:
            source, halo = (z0, halo0) if stage == 0 else (z1, halo1)
            down = (source.at[c, low_rows], halo.at[c, 1])
            up = (source.at[c, high_rows], halo.at[c, 0])
        else:
            down = (u.at[c, low_rows, pl.ds(0, half)], halo2.at[c, 1])
            up = (u.at[c, high_rows, pl.ds(half, half)], halo2.at[c, 0])
        to_low = pltpu.make_async_remote_copy(
            src_ref=down[0],
            dst_ref=down[1],
            send_sem=send_sem.at[stage, c, 0],
            recv_sem=recv_sem.at[stage, c, 1],
            device_id={"row": lax.rem(me + n - 1, n)},
            device_id_type=MESH,
        )
        to_high = pltpu.make_async_remote_copy(
            src_ref=up[0],
            dst_ref=up[1],
            send_sem=send_sem.at[stage, c, 1],
            recv_sem=recv_sem.at[stage, c, 0],
            device_id={"row": lax.rem(me + 1, n)},
            device_id_type=MESH,
        )
        return to_low, to_high

    def send(stage, c):
        to_low, to_high = exchange(stage, c)
        pl.when(me > 0)(to_low.start)
        pl.when(me < n - 1)(to_high.start)

    def receive(stage, c):
        to_low, to_high = exchange(stage, c)
        pl.when(me < n - 1)(to_low.wait_recv)
        pl.when(me > 0)(to_high.wait_recv)

    def sums(which, c):
        buffer = red0 if which == 0 else red1
        copies = []
        for k in range(1, n):
            copies.append(
                pltpu.make_async_remote_copy(
                    src_ref=buffer.at[c, me],
                    dst_ref=buffer.at[c, me],
                    send_sem=rsend_sem.at[which, c, k - 1],
                    recv_sem=rrecv_sem.at[which, c, k - 1],
                    device_id={"row": lax.rem(me + k, n)},
                    device_id_type=MESH,
                )
            )
        return copies

    def send_sums(which, c, values):
        buffer = red0 if which == 0 else red1
        for index, value in enumerate(values):
            buffer[c, me, index : index + 1, :] = value
        for copy in sums(which, c):
            copy.start()

    def receive_sums(which, c):
        for copy in sums(which, c):
            copy.wait_recv()
        buffer = red0 if which == 0 else red1
        total = buffer[c, 0]
        for source in range(1, n):
            total = total + buffer[c, source]
        return total

    def colsum(value):
        return jnp.sum(value, axis=0, keepdims=True)

    def apply_precond(c, source, target):
        for b in range(rows // block):
            at = slice(b * block, (b + 1) * block)
            high, low = split(source[c, at])
            product = dot(pcat[at], jnp.concatenate([high, high], axis=0)) + dot(
                pcat[at, 0:block], low
            )
            target[c, at] = product

    def local_image(c, source, target):
        high, low = split(source[c])
        vhi[c] = high
        vlo[c] = low
        for b in range(rows // edge):
            at = slice(b * edge, (b + 1) * edge)
            coupled = dot3(chi[at, mid_cols], clo[at, mid_cols], vhi[c], vlo[c])
            target[c, at] = diag[at] * source[c, at] - coupled

    def edge_image(c, halo, target):
        for side, at, cols in ((0, low_rows, low_cols), (1, high_rows, high_cols)):
            high, low = split(halo[c, side])
            target[c, at] = target[c, at] - dot3(chi[at, cols], clo[at, cols], high, low)

    @pl.when(me == 0)
    def _():
        for c in range(chunks):
            for halo in (halo0, halo1, halo2):
                halo[c, 0] = jnp.zeros(halo.shape[2:], F32)

    @pl.when(me == n - 1)
    def _():
        for c in range(chunks):
            for halo in (halo0, halo1, halo2):
                halo[c, 1] = jnp.zeros(halo.shape[2:], F32)

    loads[0].wait()
    high, low = split(precond[...])
    pcat[:, 0:block] = high
    pcat[:, block : 2 * block] = low
    for c in range(chunks):
        loads[1 + c].wait()
        apply_precond(c, rhs, z0)
        if c == 0:
            pl.semaphore_wait(barrier, n - 1)
        send(0, c)

    loads[-1].wait()
    reach_max = half_ref[0]
    for b in range(rows // block):
        at = slice(b * block, (b + 1) * block)
        values = band[at]
        offsets = (
            lax.broadcasted_iota(jnp.int32, values.shape, 1)
            - edge
            - b * block
            - lax.broadcasted_iota(jnp.int32, values.shape, 0)
        )
        reach = jnp.abs(offsets)
        kept = jnp.where(reach <= reach_max, values, 0.0)
        diag[at] = jnp.sum(kept, axis=1, keepdims=True)
        coupling = jnp.where(reach >= 1, kept, 0.0)
        high, low = split(coupling)
        chi[at] = high
        clo[at] = low

    for c in range(chunks):
        local_image(c, z0, w0)
    for c in range(chunks):
        receive(0, c)
        edge_image(c, halo0, w0)
        apply_precond(c, w0, z1)
        send(1, c)
        send_sums(0, c, [colsum(rhs[c] * z0[c]), colsum(z0[c] * w0[c])])
        local_image(c, z1, w1)

    first = []
    for c in range(chunks):
        receive(1, c)
        edge_image(c, halo1, w1)
        total = receive_sums(0, c)
        energy, product = total[0:1], total[1:2]
        step = energy / product
        first.append((energy, product, step))
        for b in range(rows // block):
            at = slice(b * block, (b + 1) * block)
            high, low = split(w1[c, at])
            z2 = dot(pcat[at], jnp.concatenate([high, high], axis=0)) + dot(pcat[at, 0:block], low)
            u[c, at] = z1[c, at] - step * z2
        send(2, c)

    partial = []
    for c in range(chunks):
        step = first[c][2]
        terms = None
        high, low = split(u[c])
        vhi[c] = high
        vlo[c] = low
        for b in range(rows // block):
            at = slice(b * block, (b + 1) * block)
            residual = rhs[c, at] - step * w0[c, at]
            pres = z0[c, at] - step * z1[c, at]
            image = w0[c, at] - step * w1[c, at]
            ub = u[c, at]
            coupled = dot3(chi[at, mid_cols], clo[at, mid_cols], vhi[c], vlo[c])
            new = [
                colsum(residual * pres),
                colsum(pres * image),
                colsum(ub * w0[c, at]),
                colsum(ub * residual),
                colsum(ub * image),
                colsum(ub * (diag[at] * ub - coupled)),
            ]
            terms = new if terms is None else [x + y for x, y in zip(terms, new)]
        partial.append(terms)

    for c in range(chunks):
        receive(2, c)
        sides = []
        for side, at, cols, lanes in (
            (1, high_rows, high_cols, slice(0, half)),
            (0, low_rows, low_cols, slice(half, CHUNK)),
        ):
            high, low = split(halo2[c, side])
            coupled = dot3(chi[at, cols], clo[at, cols], high, low)
            sides.append(colsum(u[c, at, lanes] * coupled))
        terms = partial[c]
        terms[5] = terms[5] - 2.0 * jnp.concatenate(sides, axis=1)
        send_sums(1, c, terms)

    stores = []
    for c in range(chunks):
        energy, product, step = first[c]
        total = receive_sums(1, c)
        energy1, image1, uw, ur, ui, uku = [total[i : i + 1] for i in range(6)]
        ratio = energy1 / energy
        product1 = image1 - ratio * energy1 / step
        step1 = energy1 / product1
        along = ui + ratio * uw
        f0 = uw / product
        f1 = along / product1
        gamma = (ur - step1 * along) / (uku - f0 * uw - f1 * along)
        rest = step1 - gamma * f1
        cz0 = -(step - gamma * f0 + rest * (1.0 + ratio))
        cz1 = step * rest
        for b in range(rows // block):
            at = slice(b * block, (b + 1) * block)
            out[c, at] = cz0 * z0[c, at] + cz1 * z1[c, at] - gamma * u[c, at]
        store = pltpu.make_async_copy(
            out.at[c], out_hbm.at[:, pl.ds(c * CHUNK, CHUNK)], out_sem.at[c]
        )
        store.start()
        stores.append(store)

    for stage in range(3):
        for c in range(chunks):
            to_low, to_high = exchange(stage, c)
            pl.when(me > 0)(to_low.wait_send)
            pl.when(me < n - 1)(to_high.wait_send)
    for which in range(2):
        for c in range(chunks):
            for copy in sums(which, c):
                copy.wait_send()
    for store in stores:
        store.wait()


def solution(mesh):
    n = mesh.shape["row"]

    def per_device(band, precond, half_band, interface):
        rows, width = band.shape
        block = precond.shape[1]
        edge = (width - rows) // 2
        cols = interface.shape[1]
        chunks = cols // CHUNK
        full = pltpu.VMEM((chunks, rows, CHUNK), F32)
        any_spec = pl.BlockSpec(memory_space=pl.ANY)
        return pl.pallas_call(
            functools.partial(kernel, n),
            out_shape=jax.ShapeDtypeStruct((rows, cols), F32),
            in_specs=[any_spec, any_spec, pl.BlockSpec(memory_space=pltpu.SMEM), any_spec],
            out_specs=any_spec,
            scratch_shapes=[
                pltpu.VMEM((rows, width), F32),
                pltpu.VMEM((rows, block), F32),
                full,
                full,
                pltpu.VMEM((rows, width), BF16),
                pltpu.VMEM((rows, width), BF16),
                pltpu.VMEM((rows, 2 * block), BF16),
                pltpu.VMEM((rows, 1), F32),
                full,
                full,
                full,
                full,
                full,
                pltpu.VMEM((chunks, rows, CHUNK), BF16),
                pltpu.VMEM((chunks, rows, CHUNK), BF16),
                pltpu.VMEM((chunks, 2, edge, CHUNK), F32),
                pltpu.VMEM((chunks, 2, edge, CHUNK), F32),
                pltpu.VMEM((chunks, 2, edge, CHUNK // 2), F32),
                pltpu.VMEM((chunks, n, 8, CHUNK), F32),
                pltpu.VMEM((chunks, n, 8, CHUNK), F32),
                pltpu.SemaphoreType.DMA((2 + chunks,)),
                pltpu.SemaphoreType.DMA((chunks,)),
                pltpu.SemaphoreType.DMA((3, chunks, 2)),
                pltpu.SemaphoreType.DMA((3, chunks, 2)),
                pltpu.SemaphoreType.DMA((2, chunks, n - 1)),
                pltpu.SemaphoreType.DMA((2, chunks, n - 1)),
            ],
            compiler_params=pltpu.CompilerParams(
                collective_id=0, has_side_effects=True, vmem_limit_bytes=48 * 1024 * 1024
            ),
        )(band, precond, half_band, interface)

    return jax.shard_map(
        per_device,
        mesh=mesh,
        in_specs=(
            P(("sub", "row"), None),
            P(("sub", "row"), None),
            P("sub"),
            P(("sub", "row"), None),
        ),
        out_specs=P(("sub", "row"), None),
        check_vma=False,
    )
```

```python
import functools

import jax
import jax.numpy as jnp
from jax import lax
from jax.experimental import pallas as pl
from jax.experimental.pallas import tpu as pltpu
from jax.sharding import PartitionSpec as P

MESH = pl.DeviceIdType.MESH
CHUNK = 256
F32 = jnp.float32
BF16 = jnp.bfloat16


def split(value):
    high = value.astype(BF16)
    return high, (value - high.astype(F32)).astype(BF16)


def dot(left, right):
    return jnp.dot(left, right, preferred_element_type=F32)


def dot3(left_hi, left_lo, right_hi, right_lo):
    return dot(left_hi, right_hi) + dot(left_lo, right_hi) + dot(left_hi, right_lo)


def kernel(
    n,
    band_hbm,
    precond_hbm,
    half_ref,
    rhs_hbm,
    out_ref,
    band,
    precond,
    rhs,
    chi,
    clo,
    pcat,
    diag,
    z0,
    w0,
    z1,
    w1,
    u,
    vhi,
    vlo,
    halo0,
    halo1,
    halo2,
    red0,
    red1,
    in_sem,
    send_sem,
    recv_sem,
    rsend_sem,
    rrecv_sem,
):
    me = lax.axis_index("row")
    rows, width = band.shape
    edge = (width - rows) // 2
    block = precond.shape[1]
    chunks = rhs.shape[0]
    half = edge // 2
    low_rows, high_rows = slice(0, edge), slice(rows - edge, rows)
    near_low, near_high = slice(0, half), slice(rows - half, rows)
    low_cols, mid_cols, high_cols = slice(0, edge), slice(edge, edge + rows), slice(edge + rows, width)

    loads = [pltpu.make_async_copy(precond_hbm, precond, in_sem.at[0])]
    for c in range(chunks):
        loads.append(
            pltpu.make_async_copy(
                rhs_hbm.at[:, pl.ds(c * CHUNK, CHUNK)], rhs.at[c], in_sem.at[2 + c]
            )
        )
    loads.append(pltpu.make_async_copy(band_hbm, band, in_sem.at[1]))
    for load in loads[:-1]:
        load.start()

    barrier = pltpu.get_barrier_semaphore()
    for k in range(1, n):
        pl.semaphore_signal(
            barrier, inc=1, device_id={"row": lax.rem(me + k, n)}, device_id_type=MESH
        )

    def exchange(stage, c):
        if stage < 2:
            source, halo = (z0, halo0) if stage == 0 else (z1, halo1)
            down = (source.at[c, low_rows], halo.at[c, 1])
            up = (source.at[c, high_rows], halo.at[c, 0])
        else:
            down = (u.at[c, near_low], halo2.at[c, 1])
            up = (u.at[c, near_high], halo2.at[c, 0])
        to_low = pltpu.make_async_remote_copy(
            src_ref=down[0],
            dst_ref=down[1],
            send_sem=send_sem.at[stage, c, 0],
            recv_sem=recv_sem.at[stage, c, 1],
            device_id={"row": lax.rem(me + n - 1, n)},
            device_id_type=MESH,
        )
        to_high = pltpu.make_async_remote_copy(
            src_ref=up[0],
            dst_ref=up[1],
            send_sem=send_sem.at[stage, c, 1],
            recv_sem=recv_sem.at[stage, c, 0],
            device_id={"row": lax.rem(me + 1, n)},
            device_id_type=MESH,
        )
        return to_low, to_high

    def send(stage, c):
        to_low, to_high = exchange(stage, c)
        pl.when(me > 0)(to_low.start)
        pl.when(me < n - 1)(to_high.start)

    def receive(stage, c):
        to_low, to_high = exchange(stage, c)
        pl.when(me < n - 1)(to_low.wait_recv)
        pl.when(me > 0)(to_high.wait_recv)

    def sums(which, c):
        buffer = red0 if which == 0 else red1
        copies = []
        for k in range(1, n):
            copies.append(
                pltpu.make_async_remote_copy(
                    src_ref=buffer.at[c, me],
                    dst_ref=buffer.at[c, me],
                    send_sem=rsend_sem.at[which, c, k - 1],
                    recv_sem=rrecv_sem.at[which, c, k - 1],
                    device_id={"row": lax.rem(me + k, n)},
                    device_id_type=MESH,
                )
            )
        return copies

    def send_sums(which, c, values):
        buffer = red0 if which == 0 else red1
        for index, value in enumerate(values):
            buffer[c, me, index : index + 1, :] = value
        for copy in sums(which, c):
            copy.start()

    def receive_sums(which, c):
        for copy in sums(which, c):
            copy.wait_recv()
        buffer = red0 if which == 0 else red1
        total = buffer[c, 0]
        for source in range(1, n):
            total = total + buffer[c, source]
        return total

    def colsum(value):
        return jnp.sum(value, axis=0, keepdims=True)

    def apply_precond(c, source, target):
        for b in range(rows // block):
            at = slice(b * block, (b + 1) * block)
            high, low = split(source[c, at])
            product = dot(pcat[at], jnp.concatenate([high, high], axis=0)) + dot(
                pcat[at, 0:block], low
            )
            target[c, at] = product

    def local_image(c, source, target):
        high, low = split(source[c])
        vhi[c] = high
        vlo[c] = low
        for b in range(rows // edge):
            at = slice(b * edge, (b + 1) * edge)
            coupled = dot3(chi[at, mid_cols], clo[at, mid_cols], vhi[c], vlo[c])
            target[c, at] = diag[at] * source[c, at] - coupled

    def edge_image(c, halo, target):
        for side, at, cols in ((0, low_rows, low_cols), (1, high_rows, high_cols)):
            high, low = split(halo[c, side])
            target[c, at] = target[c, at] - dot3(chi[at, cols], clo[at, cols], high, low)

    @pl.when(me == 0)
    def _():
        for c in range(chunks):
            for halo in (halo0, halo1, halo2):
                halo[c, 0] = jnp.zeros(halo.shape[2:], F32)

    @pl.when(me == n - 1)
    def _():
        for c in range(chunks):
            for halo in (halo0, halo1, halo2):
                halo[c, 1] = jnp.zeros(halo.shape[2:], F32)

    loads[0].wait()
    high, low = split(precond[...])
    pcat[:, 0:block] = high
    pcat[:, block : 2 * block] = low
    for c in range(chunks):
        loads[1 + c].wait()
        if c == 0:
            loads[-1].start()
        apply_precond(c, rhs, z0)
        if c == 0:
            pl.semaphore_wait(barrier, n - 1)
        send(0, c)

    loads[-1].wait()
    reach_max = half_ref[0]
    for b in range(rows // block):
        at = slice(b * block, (b + 1) * block)
        values = band[at]
        offsets = (
            lax.broadcasted_iota(jnp.int32, values.shape, 1)
            - edge
            - b * block
            - lax.broadcasted_iota(jnp.int32, values.shape, 0)
        )
        reach = jnp.abs(offsets)
        kept = jnp.where(reach <= reach_max, values, 0.0)
        diag[at] = jnp.sum(kept, axis=1, keepdims=True)
        coupling = jnp.where(reach >= 1, kept, 0.0)
        high, low = split(coupling)
        chi[at] = high
        clo[at] = low

    for c in range(chunks):
        local_image(c, z0, w0)
    for c in range(chunks):
        receive(0, c)
        edge_image(c, halo0, w0)
        apply_precond(c, w0, z1)
        send(1, c)
        send_sums(0, c, [colsum(rhs[c] * z0[c]), colsum(z0[c] * w0[c])])
        local_image(c, z1, w1)

    first = []
    for c in range(chunks):
        receive(1, c)
        edge_image(c, halo1, w1)
        total = receive_sums(0, c)
        energy, product = total[0:1], total[1:2]
        step = energy / product
        first.append((energy, product, step))
        for b in range(rows // block):
            at = slice(b * block, (b + 1) * block)
            high, low = split(w1[c, at])
            z2 = dot(pcat[at], jnp.concatenate([high, high], axis=0)) + dot(pcat[at, 0:block], low)
            u[c, at] = z1[c, at] - step * z2
        send(2, c)

    partial = []
    for c in range(chunks):
        step = first[c][2]
        terms = None
        high, low = split(u[c])
        vhi[c] = high
        vlo[c] = low
        for b in range(rows // block):
            at = slice(b * block, (b + 1) * block)
            residual = rhs[c, at] - step * w0[c, at]
            pres = z0[c, at] - step * z1[c, at]
            image = w0[c, at] - step * w1[c, at]
            ub = u[c, at]
            coupled = dot3(chi[at, mid_cols], clo[at, mid_cols], vhi[c], vlo[c])
            new = [
                colsum(residual * pres),
                colsum(pres * image),
                colsum(ub * w0[c, at]),
                colsum(ub * residual),
                colsum(ub * image),
                colsum(ub * (diag[at] * ub - coupled)),
            ]
            terms = new if terms is None else [x + y for x, y in zip(terms, new)]
        partial.append(terms)

    for c in range(chunks):
        receive(2, c)
        terms = partial[c]
        for side, at, cols in (
            (0, low_rows, slice(half, edge)),
            (1, slice(rows - edge, rows - half), slice(edge + rows, edge + rows + half)),
        ):
            high, low = split(halo2[c, side])
            coupled = dot3(chi[at, cols], clo[at, cols], high, low)
            terms[5] = terms[5] - 2.0 * colsum(u[c, at] * coupled)
        send_sums(1, c, terms)

    for c in range(chunks):
        energy, product, step = first[c]
        total = receive_sums(1, c)
        energy1, image1, uw, ur, ui, uku = [total[i : i + 1] for i in range(6)]
        ratio = energy1 / energy
        product1 = image1 - ratio * energy1 / step
        step1 = energy1 / product1
        along = ui + ratio * uw
        f0 = uw / product
        f1 = along / product1
        gamma = (ur - step1 * along) / (uku - f0 * uw - f1 * along)
        rest = step1 - gamma * f1
        cz0 = -(step - gamma * f0 + rest * (1.0 + ratio))
        cz1 = step * rest
        for b in range(rows // block):
            at = slice(b * block, (b + 1) * block)
            out_ref[at, c * CHUNK : (c + 1) * CHUNK] = (
                cz0 * z0[c, at] + cz1 * z1[c, at] - gamma * u[c, at]
            )

    for stage in range(3):
        for c in range(chunks):
            to_low, to_high = exchange(stage, c)
            pl.when(me > 0)(to_low.wait_send)
            pl.when(me < n - 1)(to_high.wait_send)
    for which in range(2):
        for c in range(chunks):
            for copy in sums(which, c):
                copy.wait_send()


def solution(mesh):
    n = mesh.shape["row"]

    def per_device(band, precond, half_band, interface):
        rows, width = band.shape
        block = precond.shape[1]
        edge = (width - rows) // 2
        cols = interface.shape[1]
        chunks = cols // CHUNK
        band, precond, interface = (
            pltpu.with_memory_space_constraint(x, pltpu.HBM) for x in (band, precond, interface)
        )
        full = pltpu.VMEM((chunks, rows, CHUNK), F32)
        any_spec = pl.BlockSpec(memory_space=pl.ANY)
        return pl.pallas_call(
            functools.partial(kernel, n),
            out_shape=pltpu.VMEM((rows, cols), F32),
            in_specs=[any_spec, any_spec, pl.BlockSpec(memory_space=pltpu.SMEM), any_spec],
            out_specs=pl.BlockSpec(memory_space=pltpu.VMEM),
            scratch_shapes=[
                pltpu.VMEM((rows, width), F32),
                pltpu.VMEM((rows, block), F32),
                full,
                pltpu.VMEM((rows, width), BF16),
                pltpu.VMEM((rows, width), BF16),
                pltpu.VMEM((rows, 2 * block), BF16),
                pltpu.VMEM((rows, 1), F32),
                full,
                full,
                full,
                full,
                full,
                pltpu.VMEM((chunks, rows, CHUNK), BF16),
                pltpu.VMEM((chunks, rows, CHUNK), BF16),
                pltpu.VMEM((chunks, 2, edge, CHUNK), F32),
                pltpu.VMEM((chunks, 2, edge, CHUNK), F32),
                pltpu.VMEM((chunks, 2, edge // 2, CHUNK), F32),
                pltpu.VMEM((chunks, n, 8, CHUNK), F32),
                pltpu.VMEM((chunks, n, 8, CHUNK), F32),
                pltpu.SemaphoreType.DMA((2 + chunks,)),
                pltpu.SemaphoreType.DMA((3, chunks, 2)),
                pltpu.SemaphoreType.DMA((3, chunks, 2)),
                pltpu.SemaphoreType.DMA((2, chunks, n - 1)),
                pltpu.SemaphoreType.DMA((2, chunks, n - 1)),
            ],
            compiler_params=pltpu.CompilerParams(
                collective_id=0, has_side_effects=True, vmem_limit_bytes=48 * 1024 * 1024
            ),
        )(band, precond, half_band, interface)

    return jax.shard_map(
        per_device,
        mesh=mesh,
        in_specs=(
            P(("sub", "row"), None),
            P(("sub", "row"), None),
            P("sub"),
            P(("sub", "row"), None),
        ),
        out_specs=P(("sub", "row"), None),
        check_vma=False,
    )
```
